256 devices in a mesh: blk: 32 (over x, z_lo, core), grp: 8 (over y, z_hi).
Axes of the slice: x: 4, y: 4, z: 8 (z_hi: 2, z_lo: 4; z = z_hi * 4 + z_lo), core: 2. Of those that a mesh axis runs over, the one named last changes fastest.
Arguments:
- activations: bfloat16 [16384, 8192], P('blk', 'grp'), may hold values from -6 to 6
- output_grads: bfloat16 [16384, 28672], P('blk', 'grp'), may hold values from -6 to 6
- query_left: bfloat16 [64, 32, 8192], P('blk', None, 'grp'), may hold values from -0.0078125 to 0.0078125
- query_right: bfloat16 [64, 32, 28672], P('blk', None, 'grp'), may hold values from -0.00390625 to 0.00390625
- basis_inputs: bfloat16 [32, 8192, 256], P('blk', 'grp'), may hold values from -0.0625 to 0.0625
- eigen_inputs: bfloat16 [32, 256], P('blk'), may hold values from 0.099609375 to 100
- basis_outputs: bfloat16 [32, 28672, 512], P('blk', 'grp'), may hold values from -0.03125 to 0.03125
- eigen_outputs: bfloat16 [32, 512], P('blk'), may hold values from 0.099609375 to 100
- owners: int32 [2], replicated, may hold values from 0 to 31
- seq_lengths: int32 [128], P('blk'), may hold values from 1 to 128, as said below
Outputs:
- scores: float32 [128, 64], P('blk')
The draws below stay inside these ranges and needn't reach their ends.
Inputs may be any that keep to these rules, and one draw needn't show every extreme that they name: `seq_lengths`: the 4 lengths of one shard sum to at most 512; in every draw some shard is full (all its lengths 128) and some sequence has length 1.
All inputs are finite; a program needn't handle non-finite values.
Results may differ from the reference program's by a relative error of at most 0.02.
Values may be sent and summed in bfloat16 or wider, within the bound.
No kernel may reach another device: no remote copies, remote signals or barrier semaphores. Data moves between devices by JAX's collectives and lax.ppermute only.
A program may use at most 128 MiB of HBM per device.

```python
import math
import jax
import jax.numpy as jnp
from jax import lax

D = 8192
F = 28672
R = 32
KA = 256
KG = 512
TOK_DEV = 512
SEQ_DEV = 4
MAXLEN = 128
SHARDS = 32
QUERIES = 64
SEQS = 128
TOKENS = 16384
N_GRP = 8


def draw_seq_lengths(key, part):
    key_lens = jax.random.fold_in(key, 11)
    key_full = jax.random.fold_in(key, 12)
    key_other = jax.random.fold_in(key, 13)
    shard_count = SEQS // SEQ_DEV
    lengths = jax.random.randint(key_lens, (shard_count, SEQ_DEV), 1, MAXLEN + 1)
    full_row = jax.random.randint(key_full, (), 0, shard_count)
    other_row = (full_row + jax.random.randint(key_other, (), 1, shard_count)) % shard_count
    row_ids = jnp.arange(shard_count, dtype=jnp.int32)[:, None]
    col_ids = jnp.arange(SEQ_DEV, dtype=jnp.int32)[None, :]
    lengths = jnp.where(row_ids == full_row, MAXLEN, lengths)
    lengths = jnp.where((row_ids == other_row) & (col_ids == 0), 1, lengths)
    return lengths.reshape(-1).astype(jnp.int32)


def level_of(rng, shape, split, low, largest):
    level = 1.0
    for dim, parts in split:
        steps = jax.random.uniform(jax.random.fold_in(jax.random.fold_in(rng, 6), dim), (parts,), jnp.float32, low / len(split), largest / len(split))
        level = level * jnp.repeat(jnp.exp(steps), shape[dim] // parts).reshape((-1,) + (1,) * (len(shape) - 1 - dim))
    return level


def bell_draw(rng, shape, spread, limit, cuts=(), kind=jnp.bfloat16):
    result = jax.random.normal(rng, shape, jnp.float32) * spread
    if len(cuts) > 0:
        result = level_of(rng, shape, cuts, -0.22, 0.18) * result
    return jnp.clip(result, min=-limit, max=limit).astype(kind)


def setup_inputs(seed: int = 0) -> dict:
    splits = jax.random.split(jax.random.key(seed), 11)
    activations = bell_draw(splits[0], (TOKENS, D), 1.0, 6.0, ((0, 32), (1, 8)))
    output_grads = bell_draw(splits[1], (TOKENS, F), 1.0, 6.0, ((0, 32), (1, 8)))
    query_left = bell_draw(splits[2], (QUERIES, R, D), (64 * D) ** -0.5, 0.0078125, ((0, 32), (2, 8)))
    query_right = bell_draw(splits[3], (QUERIES, R, F), (64 * F) ** -0.5, 0.00390625, ((0, 32), (2, 8)))
    basis_inputs = bell_draw(splits[4], (SHARDS, D, KA), D ** -0.5, 0.0625, ((0, 32), (1, 8)))
    eigen_inputs = jnp.clip(jnp.exp(math.log(100.0) - 6.9116692 * jax.random.uniform(splits[5], (SHARDS, KA), jnp.float32) ** level_of(splits[5], (SHARDS, KA), ((0, 32),), -0.2, 0.2)), 0.099609375, 100.0).astype(jnp.bfloat16)
    basis_outputs = bell_draw(splits[6], (SHARDS, F, KG), F ** -0.5, 0.03125, ((0, 32), (1, 8)))
    eigen_outputs = jnp.clip(jnp.exp(math.log(100.0) - 6.9116692 * jax.random.uniform(splits[7], (SHARDS, KG), jnp.float32) ** level_of(splits[7], (SHARDS, KG), ((0, 32),), -0.2, 0.2)), 0.099609375, 100.0).astype(jnp.bfloat16)
    owners = jax.random.randint(splits[8], (2,), 0, SHARDS).astype(jnp.int32)
    seq_lengths = draw_seq_lengths(jax.random.fold_in(splits[10], 71), 0)
    return {"activations": activations, "output_grads": output_grads, "query_left": query_left, "query_right": query_right, "basis_inputs": basis_inputs, "eigen_inputs": eigen_inputs, "basis_outputs": basis_outputs, "eigen_outputs": eigen_outputs, "owners": owners, "seq_lengths": seq_lengths}


def contract(row_block, factors):
    return lax.dot_general(row_block, factors, (((1,), (1,)), ((), ())), preferred_element_type=jnp.float32)


def precondition(factors, basis, eigen):
    flat_rows = factors.reshape(-1, factors.shape[-1])
    coeffs = jnp.dot(flat_rows, basis, preferred_element_type=jnp.float32)
    eigen_float = eigen.astype(jnp.float32)
    damped = (coeffs * (eigen_float / (1.0 + eigen_float))).astype(jnp.bfloat16)
    return (flat_rows.astype(jnp.float32) - contract(damped, basis)).astype(jnp.bfloat16)


def project(row_block, factors):
    slot_count = row_block.shape[0]
    piece_width = row_block.shape[1] // N_GRP
    left_side = row_block.astype(jnp.float32).reshape(slot_count, N_GRP, piece_width)
    right_side = factors.astype(jnp.float32).reshape(factors.shape[0], N_GRP, piece_width)
    partial_value = jnp.einsum("tgd,qgd->gtq", left_side, right_side)
    rounded = lax.optimization_barrier(partial_value.astype(jnp.bfloat16))
    return jnp.sum(rounded.astype(jnp.float32), axis=0)


def membership(seq_lens):
    seq_ends = jnp.cumsum(seq_lens).astype(jnp.int32)
    seq_starts = seq_ends - seq_lens
    position = jnp.arange(TOK_DEV, dtype=jnp.int32)[None, :]
    inside = (position >= seq_starts[:, None]) & (position < seq_ends[:, None])
    return inside.astype(jnp.float32)


def reference(activations, output_grads, query_left, query_right, basis_inputs, eigen_inputs, basis_outputs, eigen_outputs, owners, seq_lengths):
    ready_left = precondition(query_left, basis_inputs[owners[0]], eigen_inputs[owners[0]])
    ready_right = precondition(query_right, basis_outputs[owners[1]], eigen_outputs[owners[1]])
    act_shards = activations.reshape(-1, TOK_DEV, D)
    grad_shards = output_grads.reshape(-1, TOK_DEV, F)
    length_rows = seq_lengths.reshape(-1, SEQ_DEV)

    def one_shard(shard_args):
        act_rows, grad_rows, seq_lens = shard_args
        proj_left = project(act_rows, ready_left)
        proj_right = project(grad_rows, ready_right)
        token_scores = jnp.sum((proj_left * proj_right).reshape(TOK_DEV, -1, R), axis=2)
        return jnp.dot(membership(seq_lens), token_scores, precision=lax.Precision.HIGHEST, preferred_element_type=jnp.float32)

    shard_scores = lax.map(one_shard, (act_shards, grad_shards, length_rows))
    return shard_scores.reshape(-1, QUERIES)
```

```python
import jax
import jax.numpy as jnp
from jax import lax
from jax.sharding import PartitionSpec as P


NX, NZ, NC, NY, NH = 4, 4, 2, 4, 2
BF, F32 = jnp.bfloat16, jnp.float32


def blk_id(x, z, c):
    return (x * NZ + z) * NC + c


BLK = [(x, z, c) for x in range(NX) for z in range(NZ) for c in range(NC)]
GRP = [(y, h) for y in range(NY) for h in range(NH)]


def shift_x(value, step):
    pairs = [(blk_id(x, z, c), blk_id((x + step) % NX, z, c)) for x, z, c in BLK]
    return lax.ppermute(value, "blk", pairs)


def shift_z(value, step):
    pairs = [(blk_id(x, z, c), blk_id(x, (z + step) % NZ, c)) for x, z, c in BLK]
    return lax.ppermute(value, "blk", pairs)


def swap_core(value):
    pairs = [(blk_id(x, z, c), blk_id(x, z, 1 - c)) for x, z, c in BLK]
    return lax.ppermute(value, "blk", pairs)


def shift_y(value, step):
    return lax.ppermute(value, "grp", [(y * NH + h, (y + step) % NY * NH + h) for y, h in GRP])


def swap_h(value):
    return lax.ppermute(value, "grp", [(y * NH + h, y * NH + 1 - h) for y, h in GRP])


def shift_z_by_y(value):
    pairs = []
    for x, z, c in BLK:
        for y, h in GRP:
            g = y * NH + h
            pairs.append((blk_id(x, z, c) * NY * NH + g, blk_id(x, (z + y) % NZ, c) * NY * NH + g))
    return lax.ppermute(value, ("blk", "grp"), pairs)


def at(value, index):
    return lax.dynamic_index_in_dim(value, index, 0, keepdims=False)


def nt(left, right):
    return lax.dot_general(left, right, (((1,), (1,)), ((), ())), preferred_element_type=F32)


def tn(left, right):
    return lax.dot_general(left, right, (((0,), (1,)), ((), ())), preferred_element_type=F32)


def member(seq_lens, slot_count):
    seq_ends = jnp.cumsum(seq_lens)
    seq_starts = seq_ends - seq_lens
    position = jnp.arange(slot_count, dtype=jnp.int32)[None, :]
    inside = (position >= seq_starts[:, None]) & (position < seq_ends[:, None])
    return inside.astype(F32)


def put_in_order(parts, origin):
    out = jnp.zeros((len(parts),) + parts[0].shape, parts[0].dtype)
    for step, part in enumerate(parts):
        out = lax.dynamic_update_index_in_dim(out, part, (origin - step) % len(parts), 0)
    return out


def local(
    activations,
    output_grads,
    query_left,
    query_right,
    basis_inputs,
    eigen_inputs,
    basis_outputs,
    eigen_outputs,
    owners,
    seq_lengths,
):
    blk, grp = lax.axis_index("blk"), lax.axis_index("grp")
    x, z, c = blk // (NZ * NC), (blk // NC) % NZ, blk % NC
    y, h = grp // NH, grp % NH
    own_x, own_z, own_c = owners // (NZ * NC), (owners // NC) % NZ, owners % NC

    n_query, rank, d_left = query_left.shape
    d_right = query_right.shape[2]
    k_left, k_right = basis_inputs.shape[2], basis_outputs.shape[2]
    slots = activations.shape[0]
    raw_left = query_left.reshape(-1, d_left)
    raw_right = query_right.reshape(-1, d_right)
    rows = raw_left.shape[0]

    acts = (activations, swap_core(activations))
    grads = (output_grads, swap_core(output_grads))
    lens_other = swap_core(seq_lengths)
    left_both = jnp.concatenate([raw_left, swap_core(raw_left)], axis=0)
    right_both = jnp.concatenate([raw_right, swap_core(raw_right)], axis=0)

    chunks = NX * NZ
    cut_right, cut_left = d_right // chunks, d_left // chunks
    half_right, half_left = k_right // 2, k_left // 2
    strips = half_right // 128

    def pack(half):
        right = basis_outputs[0][:, half * half_right : (half + 1) * half_right]
        right = right.reshape(chunks, cut_right, strips, 128).transpose(0, 2, 1, 3)
        right = right.reshape(chunks, strips * cut_right, 128)
        left = basis_inputs[0][:, half * half_left : (half + 1) * half_left]
        left = left.reshape(chunks, cut_left, 128)
        tail = jnp.concatenate(
            [
                eigen_outputs[0, half * half_right : (half + 1) * half_right].reshape(strips, 128),
                eigen_inputs[0, half * half_left : (half + 1) * half_left].reshape(1, 128),
                jnp.zeros((16 - strips - 1, 128), BF),
            ],
            axis=0,
        )
        tail = jnp.broadcast_to(tail[None], (chunks, 16, 128))
        return jnp.concatenate([right, left, tail], axis=1)

    body_rows = strips * cut_right + cut_left
    line = jnp.arange(body_rows + 16, dtype=jnp.int32)
    of_right = (line < strips * cut_right) | ((line >= body_rows) & (line < body_rows + strips))

    def pick(coordinate, value, yes, no):
        cond = jnp.where(of_right, coordinate[1] == value, coordinate[0] == value)
        return jnp.where(cond[:, None], yes, no)

    first, second = pack(0), pack(1)
    mine = jnp.where(c == 0, first, second)
    other = swap_core(jnp.where(c == 0, second, first))
    held = pick(own_c, c, mine, other).reshape(NX, NZ, body_rows + 16, 128)
    got = at(held, x)
    for step in range(1, NX):
        moved = shift_x(at(held, (x + step) % NX), step)
        got = pick(own_x, (x - step) % NX, moved, got)
    held, got = got, at(got, z)
    for step in range(1, NZ):
        moved = shift_z(at(held, (z + step) % NZ), step)
        got = pick(own_z, (z - step) % NZ, moved, got)
    eigen = got[body_rows : body_rows + strips + 1].astype(F32)
    got = got[:body_rows]
    got = put_in_order([got] + [shift_z(got, step) for step in range(1, NZ)], z)
    got = put_in_order([got] + [shift_x(got, step) for step in range(1, NX)], x)
    got = got.reshape(chunks, body_rows, 128)
    half_basis_right = (
        got[:, : strips * cut_right]
        .reshape(chunks, strips, cut_right, 128)
        .transpose(0, 2, 1, 3)
        .reshape(d_right, half_right)
    )
    half_basis_left = got[:, strips * cut_right :].reshape(d_left, half_left)

    coord_right = jnp.concatenate([tn(half_basis_right, v) for v in (*grads, right_both)], axis=1)
    coord_left = jnp.concatenate([tn(half_basis_left, v) for v in (*acts, left_both)], axis=1)
    width = coord_right.shape[1]
    quarter_right, quarter_left = half_right // NY, half_left // NY
    coord = jnp.concatenate(
        [
            coord_right.astype(BF).reshape(NY, quarter_right, width),
            coord_left.astype(BF).reshape(NY, quarter_left, width),
        ],
        axis=1,
    )
    total = at(coord, y).astype(F32)
    for step in range(1, NY):
        total = total + shift_y(at(coord, (y + step) % NY), step).astype(F32)
    total = total.astype(BF)
    total = total.astype(F32) + swap_h(total).astype(F32)
    factor = eigen / (1.0 + eigen)
    factor = jnp.concatenate(
        [factor[:strips].reshape(NY, quarter_right), factor[strips:].reshape(NY, quarter_left)], axis=1
    )
    is_query = jnp.arange(width, dtype=jnp.int32)[None, :] >= 2 * slots
    total = jnp.where(is_query, total * at(factor, y)[:, None], total).astype(BF)
    coord = jnp.stack([total] + [shift_y(total, step) for step in range(1, NY)])
    coord_other = swap_core(coord)

    def split(value):
        return value[:, :quarter_right].reshape(-1, width), value[:, quarter_right:].reshape(-1, width)

    here_right, here_left = split(coord)
    there_right, there_left = split(coord_other)

    def token_part(here, there):
        swapped = jnp.concatenate([there[:, slots : 2 * slots], there[:, :slots]], axis=1)
        return jnp.concatenate([here[:, : 2 * slots], swapped], axis=0)

    def query_part(here, there):
        return jnp.concatenate(
            [here[:, 2 * slots : 2 * slots + rows], there[:, 2 * slots + rows :]], axis=0
        ).T

    damped = jnp.concatenate(
        [query_part(here_right, there_right), query_part(here_left, there_left)], axis=1
    ).reshape(n_query, rank, k_right + k_left)
    damped = shift_z_by_y(at(damped, h))
    damped = jnp.concatenate([damped] + [shift_x(damped, step) for step in range(1, NX)], axis=0)
    fix_right = jnp.dot(
        damped[:, :k_right], token_part(here_right, there_right), preferred_element_type=F32
    )
    fix_left = jnp.dot(
        damped[:, k_right:], token_part(here_left, there_left), preferred_element_type=F32
    )

    right_own = jnp.concatenate(
        [raw_right] + [shift_z(raw_right, step) for step in range(1, NZ)], axis=0
    )
    right_prev, right_next = shift_x(right_own, 1), shift_x(right_own, -1)
    cut = right_own.shape[0] // 2
    right_far = jnp.concatenate(
        [shift_x(right_prev[:cut], 1), shift_x(right_next[cut:], -1)], axis=0
    )
    right_all = (right_own, right_prev, right_far, right_next)
    left_row = jnp.concatenate(
        [raw_left] + [shift_x(raw_left, step) for step in range(1, NX)], axis=0
    )
    left_rows = [left_row] + [shift_z(left_row, step) for step in range(1, NZ)]
    left_all = [
        jnp.concatenate([v[d * rows : (d + 1) * rows] for v in left_rows], axis=0) for d in range(NX)
    ]

    def project(d):
        right = jnp.concatenate([nt(right_all[d], v).astype(BF) for v in grads], axis=1)
        left = jnp.concatenate([nt(left_all[d], v).astype(BF) for v in acts], axis=1)
        return [v.reshape(NY, 1, rows, 2 * slots) for v in (left, right)]

    sums = {}
    for group in ((0,), (1, 3), (2,)):
        parts = [p for d in group for p in project(d)]
        parts = jnp.concatenate(parts, axis=1)
        total = at(parts, y).astype(F32)
        for step in range(1, NY):
            total = total + shift_y(at(parts, (y + step) % NY), step).astype(F32)
        total = total.astype(BF).reshape(2 * len(group), NH, rank, 2 * slots)
        keep = lax.dynamic_index_in_dim(total, h, 1, keepdims=False)
        give = lax.dynamic_index_in_dim(total, 1 - h, 1, keepdims=False)
        total = keep.astype(F32) + swap_h(give).astype(F32)
        for i, d in enumerate(group):
            sums[d] = total[2 * i], total[2 * i + 1]

    token_scores = []
    for d in range(NX):
        part = slice(d * rank, (d + 1) * rank)
        token_scores.append(
            jnp.sum((sums[d][0] - fix_left[part]) * (sums[d][1] - fix_right[part]), axis=0)
        )
    token_scores = jnp.stack(token_scores)

    def by_sequence(lens, scores):
        return lax.dot_general(
            member(lens, slots),
            scores,
            (((1,), (1,)), ((), ())),
            precision=lax.Precision.HIGHEST,
            preferred_element_type=F32,
        )

    part = by_sequence(seq_lengths, token_scores[:, :slots])
    part_other = swap_core(by_sequence(lens_other, token_scores[:, slots:]))
    part = jnp.concatenate([part, part_other], axis=1)
    part = jnp.concatenate([part, swap_h(part)], axis=1)
    part = jnp.concatenate([part] + [shift_y(part, step) for step in range(1, NY)], axis=1)
    n_out = part.shape[1]
    index = jnp.arange(n_out, dtype=jnp.int32)
    dx, dc, dh, dy = index % 4, (index // 4) % 2, (index // 8) % 2, index // 16
    column = (
        ((x - dx) % NX) * 16 + ((z - y + dy) % NZ) * 4 + ((c + dc) % NC) * 2 + (h + dh) % NH
    )
    place = (column[:, None] == jnp.arange(n_out, dtype=jnp.int32)[None, :]).astype(F32)
    return jnp.dot(part, place, precision=lax.Precision.HIGHEST, preferred_element_type=F32)


def solution(mesh):
    in_specs = (
        P("blk", "grp"),
        P("blk", "grp"),
        P("blk", None, "grp"),
        P("blk", None, "grp"),
        P("blk", "grp", None),
        P("blk", None),
        P("blk", "grp", None),
        P("blk", None),
        P(),
        P("blk"),
    )
    out_specs = P("blk", None)
    return jax.shard_map(local, mesh=mesh, in_specs=in_specs, out_specs=out_specs, check_vma=False)
```

```python
import functools

import jax
import jax.numpy as jnp
from jax import lax
from jax.experimental import pallas as pl
from jax.experimental.pallas import tpu as pltpu
from jax.sharding import PartitionSpec as P


NX, NZ, NC, NY, NH = 4, 4, 2, 4, 2
BF, F32 = jnp.bfloat16, jnp.float32


def blk_id(x, z, c):
    return (x * NZ + z) * NC + c


BLK = [(x, z, c) for x in range(NX) for z in range(NZ) for c in range(NC)]
GRP = [(y, h) for y in range(NY) for h in range(NH)]


def shift_x(value, step):
    pairs = [(blk_id(x, z, c), blk_id((x + step) % NX, z, c)) for x, z, c in BLK]
    return lax.ppermute(value, "blk", pairs)


def shift_z(value, step):
    pairs = [(blk_id(x, z, c), blk_id(x, (z + step) % NZ, c)) for x, z, c in BLK]
    return lax.ppermute(value, "blk", pairs)


def swap_core(value):
    pairs = [(blk_id(x, z, c), blk_id(x, z, 1 - c)) for x, z, c in BLK]
    return lax.ppermute(value, "blk", pairs)


def shift_y(value, step):
    pairs = [(y * NH + h, (y + step) % NY * NH + h) for y, h in GRP]
    return lax.ppermute(value, "grp", pairs)


def swap_h(value):
    return lax.ppermute(value, "grp", [(y * NH + h, y * NH + 1 - h) for y, h in GRP])


def shift_x_by_y(value, step):
    pairs = []
    for x, z, c in BLK:
        for y, h in GRP:
            g = y * NH + h
            to = blk_id((x + y) % NX, (z + step) % NZ, c)
            pairs.append((blk_id(x, z, c) * NY * NH + g, to * NY * NH + g))
    return lax.ppermute(value, ("blk", "grp"), pairs)


def at(value, index):
    return lax.dynamic_index_in_dim(value, index, 0, keepdims=False)


def nt(left, right):
    return lax.dot_general(left, right, (((1,), (1,)), ((), ())), preferred_element_type=F32)


def member(seq_lens, slot_count):
    seq_ends = jnp.cumsum(seq_lens)
    seq_starts = seq_ends - seq_lens
    position = jnp.arange(slot_count, dtype=jnp.int32)[None, :]
    inside = (position >= seq_starts[:, None]) & (position < seq_ends[:, None])
    return inside.astype(F32)


def put_in_order(parts, origin):
    out = jnp.zeros((len(parts),) + parts[0].shape, parts[0].dtype)
    for step, part in enumerate(parts):
        out = lax.dynamic_update_index_in_dim(out, part, (origin + (4 - step)) & 3, 0)
    return out


GROUPS = ((0,), (1, 2), (3,))


def whole(value):
    return pl.BlockSpec(value.shape, lambda *_: (0,) * value.ndim)


def project_body(n_slots, y_ref, *refs):
    factors = refs[: n_slots * NX]
    tokens = refs[n_slots * NX : n_slots * NX + 4]
    outs = refs[n_slots * NX + 4 : n_slots * NX + 4 + NY]
    acc = refs[-1]
    step = pl.program_id(0)
    rows = factors[0].shape[0]
    slots, left = tokens[0].shape
    wide = tokens[2].shape[1]

    def flush(side):
        for k in range(NY):
            y_to = (y_ref[0] + k) & 3
            for n in range(n_slots):
                start = pl.multiple_of((n * NX + y_to) * rows, rows)
                outs[k][side * n_slots + n] = acc[pl.ds(start, rows), :].astype(BF)

    @pl.when(step == 0)
    def _():
        factor = jnp.concatenate([f[:, :left] for f in factors], axis=0)
        for i, ref in enumerate(tokens[:2]):
            acc[:, i * slots : (i + 1) * slots] = nt(factor, ref[...])
        flush(0)
        acc[...] = jnp.zeros_like(acc)

    @pl.when(step > 0)
    def _():
        part = pl.ds(pl.multiple_of(left + (step - 1) * wide, 128), wide)
        factor = jnp.concatenate([f[:, part] for f in factors], axis=0)
        for i, ref in enumerate(tokens[2:]):
            acc[:, i * slots : (i + 1) * slots] += nt(factor, ref[...])

    @pl.when(step == pl.num_programs(0) - 1)
    def _():
        flush(1)


def project(y, factors, acts_both, grads_both):
    n_slots = len(factors) // NX
    rows, width = factors[0].shape
    slots, d_left = acts_both[0].shape
    d_right = grads_both[0].shape[1]
    left = pl.BlockSpec((slots, d_left), lambda i, _: (0, 0))
    right = pl.BlockSpec((slots, d_right // NX), lambda i, _: (0, jnp.maximum(i - 1, 0)))
    out = pl.BlockSpec((2 * n_slots, rows, 2 * slots), lambda i, _: (0, 0, 0))
    return pl.pallas_call(
        functools.partial(project_body, n_slots),
        out_shape=[jax.ShapeDtypeStruct((2 * n_slots, rows, 2 * slots), BF)] * NY,
        grid_spec=pltpu.PrefetchScalarGridSpec(
            num_scalar_prefetch=1,
            grid=(1 + NX,),
            in_specs=[whole(f) for f in factors] + [left, left, right, right],
            out_specs=[out] * NY,
            scratch_shapes=[pltpu.VMEM((len(factors) * rows, 2 * slots), F32)],
        ),
        cost_estimate=pl.CostEstimate(
            flops=2 * len(factors) * rows * 2 * slots * width,
            bytes_accessed=2 * (len(factors) * rows * width + 2 * slots * width),
            transcendentals=0,
        ),
        compiler_params=pltpu.CompilerParams(vmem_limit_bytes=40 * 1024 * 1024),
    )(y.astype(jnp.int32).reshape(1), *factors, *acts_both, *grads_both)


def nn(left, right):
    return jnp.dot(left, right, preferred_element_type=F32)


def coord_body(at_ref, *refs):
    parts, (q0, q1) = refs[:NX], refs[NX : NX + 2]
    low, high, grads = refs[NX + 2 : NX + 4], refs[NX + 4 : NX + 6], refs[NX + 6 : NX + 8]
    outs, acc = refs[NX + 8 : NX + 8 + NY], refs[-1]
    step = pl.program_id(0)
    slots, wide = grads[0].shape
    narrow = low[0].shape[1]
    rows = q0.shape[0]
    d_left = 2 * NX * narrow
    n_z, body, k_right = parts[0].shape
    cut = wide // n_z
    where = (at_ref[0] + NX - step) & 3

    @pl.when(step == 0)
    def _():
        acc[...] = jnp.zeros_like(acc)

    def columns(start, width):
        return pl.ds(pl.multiple_of(start, 128), width)

    def add(part):
        right = part[:, :cut, :].reshape(n_z * cut, k_right)
        left = part[:, cut:, :].reshape(n_z * (body - cut), k_right)
        for i in range(2):
            span = slice(i * slots, (i + 1) * slots)
            acc[span, :k_right] += nn(grads[i][...], right)
            acc[span, k_right:] += nn(low[i][...], left[:, :narrow]) + nn(high[i][...], left[:, narrow:])
        for i, q in enumerate((q0, q1)):
            span = slice(2 * slots + i * rows, 2 * slots + (i + 1) * rows)
            acc[span, :k_right] += nn(q[:, columns(d_left + where * wide, wide)], right)
            acc[span, k_right:] += nn(q[:, columns(where * narrow, narrow)], left[:, :narrow]) + nn(
                q[:, columns(d_left // 2 + where * narrow, narrow)], left[:, narrow:]
            )

    for d in range(NX):

        @pl.when(step == d)
        def _():
            add(parts[d])

    @pl.when(step == NX - 1)
    def _():
        for k in range(NY):
            y_to = (at_ref[1] + k) & 3
            start = 0
            for base, size in ((0, slots // NY), (slots, slots // NY), (2 * slots, rows // NY), (2 * slots + rows, rows // NY)):
                first = pl.multiple_of(base + y_to * size, size)
                outs[k][start : start + size, :] = acc[pl.ds(first, size), :].astype(BF)
                start += size


def coordinates(x, y, parts, queries, acts_both, grads_both):
    slots, d_left = acts_both[0].shape
    wide, narrow = grads_both[0].shape[1] // NX, d_left // (2 * NX)
    rows, width = queries[0].shape
    k_right = parts[0].shape[2]
    total = 2 * (slots + rows)

    def column(offset):
        return lambda i, ref: (0, offset + ((ref[0] + NX - i) & 3))

    low = pl.BlockSpec((slots, narrow), column(0))
    high = pl.BlockSpec((slots, narrow), column(NX))
    right = pl.BlockSpec((slots, wide), column(0))
    out = jax.ShapeDtypeStruct((total // NY, k_right + narrow), BF)
    call = pl.pallas_call(
        coord_body,
        out_shape=[out] * NY,
        grid_spec=pltpu.PrefetchScalarGridSpec(
            num_scalar_prefetch=1,
            grid=(NX,),
            in_specs=[whole(v) for v in (*parts, *queries)] + [low, low, high, high, right, right],
            out_specs=[whole(out)] * NY,
            scratch_shapes=[pltpu.VMEM((total, k_right + narrow), F32)],
        ),
        cost_estimate=pl.CostEstimate(
            flops=2 * total * (NX * wide * k_right + d_left * narrow),
            bytes_accessed=2 * (total * width + NX * wide * k_right),
            transcendentals=0,
        ),
        compiler_params=pltpu.CompilerParams(vmem_limit_bytes=40 * 1024 * 1024),
    )
    where = jnp.stack([x, y]).astype(jnp.int32)
    return call(where, *parts, *queries, *acts_both, *acts_both, *grads_both)


def score_body(n_right, y_ref, damped, here, there, *refs):
    sums, out, fix_left, fix_right = refs[:-3], refs[-3], refs[-2], refs[-1]
    size = here.shape[2]
    quarter = fix_left.shape[1] // (2 * NY)
    mine, other = damped[:, :size], damped[:, size:]

    def fix(s, a, b):
        h, t = here[s, a : a + quarter, :], there[s, b : b + quarter, :]
        return (
            nt(mine[:, n_right:], h[:, n_right:]) + nt(other[:, n_right:], t[:, n_right:]),
            nt(mine[:, :n_right], h[:, :n_right]) + nt(other[:, :n_right], t[:, :n_right]),
        )

    for s in range(NY):
        for half, (a, b) in enumerate(((0, quarter), (quarter, 0))):
            first = (half * NY + ((y_ref[0] + NY - s) & 3)) * quarter
            span = pl.ds(pl.multiple_of(first, quarter), quarter)
            fix_left[:, span], fix_right[:, span] = fix(s, a, b)
    n = 0
    for keep, give in zip(sums[0::2], sums[1::2]):
        size = keep.shape[0] // 2
        rank = keep.shape[1]
        for i in range(size):
            part = slice(n * rank, (n + 1) * rank)
            left = keep[i].astype(F32) + give[i].astype(F32) - fix_left[part]
            right = keep[size + i].astype(F32) + give[size + i].astype(F32) - fix_right[part]
            out[n : n + 1] = jnp.sum(left * right, axis=0, keepdims=True)
            n += 1


def token_scores_of(y, n_right, damped, here, there, sums):
    tokens = sums[0].shape[2]
    args = (damped, here, there, *sums)
    out = jax.ShapeDtypeStruct((NZ, tokens), F32)
    return pl.pallas_call(
        functools.partial(score_body, n_right),
        out_shape=out,
        grid_spec=pltpu.PrefetchScalarGridSpec(
            num_scalar_prefetch=1,
            grid=(1,),
            in_specs=[whole(v) for v in args],
            out_specs=whole(out),
            scratch_shapes=[pltpu.VMEM((damped.shape[0], tokens), F32)] * 2,
        ),
        cost_estimate=pl.CostEstimate(flops=10**8, bytes_accessed=4 * 10**6, transcendentals=0),
        compiler_params=pltpu.CompilerParams(vmem_limit_bytes=40 * 1024 * 1024),
    )(y.astype(jnp.int32).reshape(1), *args)


def local(
    activations,
    output_grads,
    query_left,
    query_right,
    basis_inputs,
    eigen_inputs,
    basis_outputs,
    eigen_outputs,
    owners,
    seq_lengths,
):
    return scores_of(
        activations,
        output_grads,
        query_left,
        query_right,
        basis_inputs[0],
        eigen_inputs[0],
        basis_outputs[0],
        eigen_outputs[0],
        owners,
        seq_lengths,
    )


def scores_of(
    acts, grads, query_left, query_right, basis_left, eigen_left, basis_right, eigen_right, owners, lens
):
    blk = lax.axis_index("blk").astype(jnp.uint32)
    grp = lax.axis_index("grp").astype(jnp.uint32)
    owner = owners.astype(jnp.uint32)
    x, z, c = blk >> 3, (blk >> 1) & 3, blk & 1
    y, h = grp >> 1, grp & 1
    own_x, own_z, own_c = owner >> 3, (owner >> 1) & 3, owner & 1

    _, rank, d_left = query_left.shape
    d_right = query_right.shape[2]
    k_left, k_right = basis_left.shape[1], basis_right.shape[1]
    slots = acts.shape[0]
    query = jnp.concatenate(
        [query_left.reshape(-1, d_left), query_right.reshape(-1, d_right)], axis=1
    )
    rows = query.shape[0]

    own = [query] + [shift_z(query, step) for step in range(1, NZ)]
    prev = [shift_x(v, 1) for v in own]
    following = [shift_x(v, -1) for v in own]
    far = [shift_x(prev[i], 1) if i % 2 == 0 else shift_x(following[i], -1) for i in range(NZ)]
    factors = list(zip(own, prev, far, following))

    chunks = NX * NZ
    cut_right, cut_left = d_right // chunks, d_left // chunks // 2
    half_right, half_left = k_right // 2, k_left // 2
    body, tail = cut_right + cut_left, 16

    def pack(take_first):
        def half(value, size):
            return jnp.where(take_first, value[..., :size], value[..., size:])

        right = half(basis_right, half_right).reshape(chunks, cut_right, half_right)
        left = half(basis_left, half_left)
        left = jnp.concatenate([left[: d_left // 2], left[d_left // 2 :]], axis=1)
        left = left.reshape(chunks, cut_left, half_right)
        extra = jnp.stack(
            [
                half(eigen_right, half_right),
                jnp.pad(half(eigen_left, half_left), (0, half_right - half_left)),
            ]
        )
        extra = jnp.pad(extra, ((0, tail - 2), (0, 0)))
        extra = jnp.broadcast_to(extra[None], (chunks, tail, half_right))
        return jnp.concatenate([right, left, extra], axis=1)

    line = jnp.arange(body + tail, dtype=jnp.int32)
    of_right = (line < cut_right) | (line == body)

    def pick(coordinate, value, yes, no):
        cond = jnp.where(of_right, coordinate[1] == value, coordinate[0] == value)
        return jnp.where(cond[:, None], yes, no)

    other = swap_core(pack(c == 1))
    held = pick(own_c, c, pack(c == 0), other).reshape(NX, NZ, body + tail, half_right)
    got = at(held, x)
    for step in range(1, NX):
        moved = shift_x(at(held, (x + step) & 3), step)
        got = pick(own_x, (x + (4 - step)) & 3, moved, got)
    held, got = got, at(got, z)
    for step in range(1, NZ):
        moved = shift_z(at(held, (z + step) & 3), step)
        got = pick(own_z, (z + (4 - step)) & 3, moved, got)
    eigen = got[body : body + 2].astype(F32)
    got = got[:body]
    got = put_in_order([got] + [shift_z(got, step) for step in range(1, NZ)], z)
    parts = [got] + [shift_x(got, step) for step in range(1, NX)]

    acts_both = (acts, swap_core(acts))
    grads_both = (grads, swap_core(grads))
    queries = (query, swap_core(query))

    pieces = coordinates(x, y, parts, queries, acts_both, grads_both)
    moved = [shift_y(pieces[step], step) for step in range(1, NY)]
    total = pieces[0].astype(F32)
    for v in moved:
        total = total + v.astype(F32)
    total = total.astype(BF)
    total = total.astype(F32) + swap_h(total).astype(F32)
    factor = eigen / (1.0 + eigen)
    factor = jnp.concatenate([factor[0], factor[1, :half_left]])
    quarter, few = slots // NY, rows // NY
    is_query = jnp.arange(total.shape[0], dtype=jnp.int32)[:, None] >= 2 * quarter
    total = jnp.where(is_query, total * factor[None, :], total).astype(BF)
    here = jnp.stack([total] + [shift_y(total, step) for step in range(1, NY)])
    there = swap_core(here)

    def damped_rows(y_from):
        s = (y + 4 - y_from) & 3
        return jnp.concatenate(
            [at(here, s)[2 * quarter : 2 * quarter + few], at(there, s)[2 * quarter + few :]], axis=1
        )

    damped = jnp.concatenate([damped_rows(2 * h), damped_rows(2 * h + 1)], axis=0)
    damped = jnp.concatenate([shift_x_by_y(damped, j) for j in range(NZ)], axis=0)

    sums = []
    for group in GROUPS:
        size = len(group)
        pieces = project(y, [f for d in group for f in factors[d]], acts_both, grads_both)
        moved = [shift_y(pieces[step], step) for step in range(1, NY)]
        total = pieces[0].astype(F32)
        for v in moved:
            total = total + v.astype(F32)
        total = total.astype(BF).reshape(2 * size, NH, rank, 2 * slots)
        keep = lax.dynamic_index_in_dim(total, h, 1, keepdims=False)
        give = lax.dynamic_index_in_dim(total, 1 - h, 1, keepdims=False)
        sums += [keep, swap_h(give)]

    token_scores = token_scores_of(y, half_right, damped, here, there, sums)
    token_scores = jnp.concatenate(
        [token_scores[:, :slots], swap_core(token_scores[:, slots:])], axis=0
    )
    part = lax.dot_general(
        member(lens, slots),
        token_scores,
        (((1,), (1,)), ((), ())),
        precision=lax.Precision.HIGHEST,
        preferred_element_type=F32,
    )
    part = jnp.concatenate([part, swap_h(part)], axis=1)
    part = jnp.concatenate([part] + [shift_y(part, step) for step in range(1, NY)], axis=1)
    n_out = part.shape[1]
    index = jnp.arange(n_out, dtype=jnp.uint32)
    dz, dc, dh, dy = index & 3, (index >> 2) & 1, (index >> 3) & 1, index >> 4
    column = (((x + 4 - y + dy) & 3) << 4) + (((z + 4 - dz) & 3) << 2) + ((c ^ dc) << 1) + (h ^ dh)
    place = (column[:, None] == jnp.arange(n_out, dtype=jnp.uint32)[None, :]).astype(F32)
    return jnp.dot(part, place, precision=lax.Precision.HIGHEST, preferred_element_type=F32)


def solution(mesh):
    in_specs = (
        P("blk", "grp"),
        P("blk", "grp"),
        P("blk", None, "grp"),
        P("blk", None, "grp"),
        P("blk", "grp", None),
        P("blk", None),
        P("blk", "grp", None),
        P("blk", None),
        P(),
        P("blk"),
    )
    out_specs = P("blk", None)
    return jax.shard_map(local, mesh=mesh, in_specs=in_specs, out_specs=out_specs, check_vma=False)
```
